256 devices in a mesh: ctx: 64 (over y, z_lo, x, core), head: 4 (over z_hi).
Axes of the slice: x: 4, y: 4, z: 8 (z_hi: 4, z_lo: 2; z = z_hi * 2 + z_lo), core: 2. Of those that a mesh axis runs over, the one named last changes fastest.
Arguments:
- attn_q: bfloat16 [32768, 2048], P(('ctx', 'head')), may hold values from -6 to 6
- attn_k: bfloat16 [32768, 2048], P(('ctx', 'head')), may hold values from -6 to 6
- attn_v: bfloat16 [32768, 2048], P(('ctx', 'head')), may hold values from -6 to 6
- step_size: float32 [4, 32768], P('head', 'ctx'), may hold values from 0.05 to 1
- fast_init: float32 [4, 3, 512, 512], P('head'), may hold values from -0.25 to 0.25
- boundary: int32 [1], replicated, may hold values from 8192 to 24575
- window_len: int32 [16], replicated, may hold values from 2 to 128, as said below
Outputs:
- layer_out: bfloat16 [32768, 2048], P('ctx', 'head')
The draws below stay inside these ranges and needn't reach their ends.
Inputs may be any that keep to these rules, and one draw needn't show every extreme that they name: `window_len`: some attention head has a window of exactly 128.
All inputs are finite; a program needn't handle non-finite values.
Results may differ from the reference program's by a relative error of at most 0.017.
Values may be sent and summed in bfloat16 or wider, within the bound.
No kernel may reach another device: no remote copies, remote signals or barrier semaphores. Data moves between devices by JAX's collectives and lax.ppermute only.
A program may use at most 64 MiB of HBM per device.

```python
import math
import jax
import jax.numpy as jnp
from jax import lax

D = 2048
FW = 512
AH = 128
WIN = 128
NS_STEPS = 2
NA = 16
FH = 4
TOKENS = 32768


def query_key_pair(key):
    base_q = jax.random.truncated_normal(jax.random.fold_in(key, 11), -6.0, 6.0, (TOKENS, D), jnp.float32)
    base_k = jax.random.truncated_normal(jax.random.fold_in(key, 12), -6.0, 6.0, (TOKENS, D), jnp.float32)
    return (base_q, base_k)


def draw_attn_q(key, part):
    return query_key_pair(key)[0].astype(jnp.bfloat16)


def draw_attn_k(key, part):
    return query_key_pair(key)[1].astype(jnp.bfloat16)


def draw_window_len(key, part):
    lengths = jax.random.randint(jax.random.fold_in(key, 21), (NA,), 2, WIN + 1, dtype=jnp.int32)
    widest = jax.random.randint(jax.random.fold_in(key, 22), (), 0, NA, dtype=jnp.int32)
    return jnp.where(jnp.arange(NA, dtype=jnp.int32) == widest, WIN, lengths).astype(jnp.int32)


def block_scale(key, extent, cuts, low, high):
    def one(dim, shards_of):
        heights = jax.random.uniform(jax.random.fold_in(jax.random.fold_in(key, 6), dim), (shards_of,), jnp.float32, low / len(cuts), high / len(cuts))
        return jnp.repeat(jnp.exp(heights), extent[dim] // shards_of).reshape((-1,) + (1,) * (len(extent) - dim - 1))

    gain = one(*cuts[0])
    for cut in cuts[1:]:
        gain = gain * one(*cut)
    return gain


def normal_values(rng, dims, scale, bound, cuts=(), kind=jnp.bfloat16):
    drawn = jax.random.normal(rng, dims, jnp.float32) * scale
    if len(cuts) > 0:
        drawn = block_scale(rng, dims, cuts, -0.22, 0.18) * drawn
    return jnp.clip(drawn, min=-bound, max=bound).astype(kind)


def setup_inputs(seed: int = 0) -> dict:
    splits = jax.random.split(jax.random.key(seed), 8)
    return {
        "attn_q": draw_attn_q(jax.random.fold_in(splits[7], 71), 0),
        "attn_k": draw_attn_k(jax.random.fold_in(splits[7], 71), 0),
        "attn_v": normal_values(splits[2], (TOKENS, D), 1.0, 6.0, ((0, 256),)),
        "step_size": jnp.clip(jnp.exp(math.log(1.0) - 2.9957323 * jax.random.uniform(splits[3], (FH, TOKENS), jnp.float32) ** block_scale(splits[3], (FH, TOKENS), ((0, 4), (1, 64)), -0.2, 0.2)), 0.05, 1.0),
        "fast_init": normal_values(splits[4], (FH, 3, FW, FW), FW ** -0.5, 0.25, ((0, 4),), jnp.float32),
        "boundary": jax.random.randint(splits[5], (1,), TOKENS // 4, 3 * TOKENS // 4).astype(jnp.int32),
        "window_len": draw_window_len(jax.random.fold_in(splits[7], 71), 0),
    }


ns_linear = 3.4445
ns_cubic = -4.775
ns_quintic = 2.0315

def rms_norm(values):
    x_wide = values.astype(jnp.float32)
    return x_wide / jnp.sqrt(lax.optimization_barrier(jnp.mean(x_wide * x_wide, axis=-1, keepdims=True)) + 1e-06)

def attend_rows(scores, q_pos, k_pos, window_len, v_blk):
    pos_gap = q_pos[:, None] - k_pos[None, :]
    allowed = (pos_gap[None] >= 0) & (pos_gap[None] < window_len[:, None, None]) & (k_pos[None, None, :] >= 0)
    masked = jnp.where(allowed, scores, -jnp.inf)
    row_peak = lax.optimization_barrier(jnp.max(masked, axis=-1, keepdims=True))
    expo_val = jnp.exp(masked - row_peak)
    weights_bf = (expo_val / lax.optimization_barrier(jnp.sum(expo_val, axis=-1, keepdims=True))).astype(jnp.bfloat16)
    mixed = jnp.einsum('hqk,khd->qhd', weights_bf.astype(jnp.float32), v_blk)
    return mixed.astype(jnp.bfloat16)

def window_attention(queries, key_rows, value_rows, window_len):
    zero_pad = jnp.zeros((WIN, D), jnp.bfloat16)
    keys_pad = jnp.concatenate([zero_pad, key_rows], axis=0)
    values_pad = jnp.concatenate([zero_pad, value_rows], axis=0)

    def one_block(block_id):
        row_start = block_id * WIN
        q_blk = lax.dynamic_slice_in_dim(queries, row_start, WIN, 0).reshape(WIN, NA, AH).astype(jnp.float32)
        k_blk = lax.dynamic_slice_in_dim(keys_pad, row_start, 2 * WIN, 0).reshape(2 * WIN, NA, AH).astype(jnp.float32)
        v_blk = lax.dynamic_slice_in_dim(values_pad, row_start, 2 * WIN, 0).reshape(2 * WIN, NA, AH).astype(jnp.float32)
        scores = jnp.einsum('qhd,khd->hqk', q_blk, k_blk) / math.sqrt(AH)
        q_pos = row_start + jnp.arange(WIN, dtype=jnp.int32)
        k_pos = row_start - WIN + jnp.arange(2 * WIN, dtype=jnp.int32)
        return attend_rows(scores, q_pos, k_pos, window_len, v_blk).reshape(WIN, D)
    blocks = lax.map(one_block, jnp.arange(TOKENS // WIN, dtype=jnp.int32))
    return blocks.reshape(TOKENS, D)

def swiglu_grads(fast_k, fast_v, token_scale, weights):
    w_bf = weights.astype(jnp.bfloat16)
    pre_gate = jnp.dot(fast_k, w_bf[0], preferred_element_type=jnp.float32)
    pre_up = jnp.dot(fast_k, w_bf[1], preferred_element_type=jnp.float32)
    gate_sig = jax.nn.sigmoid(pre_gate)
    gate_act = pre_gate * gate_sig
    hidden = (gate_act * pre_up).astype(jnp.bfloat16)
    target = (fast_v.astype(jnp.float32) * token_scale[:, None]).astype(jnp.bfloat16)
    grad_down = jnp.dot(hidden.T, target, preferred_element_type=jnp.float32)
    back_out = jnp.dot(target, w_bf[2].T, preferred_element_type=jnp.float32)
    back_gate = (back_out * pre_up * gate_sig * (1.0 + pre_gate * (1.0 - gate_sig))).astype(jnp.bfloat16)
    back_up = (back_out * gate_act).astype(jnp.bfloat16)
    grad_gate = jnp.dot(fast_k.T, back_gate, preferred_element_type=jnp.float32)
    grad_up = jnp.dot(fast_k.T, back_up, preferred_element_type=jnp.float32)
    return jnp.stack([grad_gate, grad_up, grad_down])

def swiglu_apply(fast_q, weights):
    w_bf = weights.astype(jnp.bfloat16)
    pre_gate = jnp.dot(fast_q, w_bf[0], preferred_element_type=jnp.float32)
    pre_up = jnp.dot(fast_q, w_bf[1], preferred_element_type=jnp.float32)
    hidden = (pre_gate * jax.nn.sigmoid(pre_gate) * pre_up).astype(jnp.bfloat16)
    return jnp.dot(hidden, w_bf[2], preferred_element_type=jnp.float32)

def newton_schulz(grad_sum):
    norm_sq = lax.optimization_barrier(jnp.sum(grad_sum * grad_sum, axis=(1, 2)))
    ortho_bf = (grad_sum / (jnp.sqrt(norm_sq) + 1e-07)[:, None, None]).astype(jnp.bfloat16)
    for ns_step in range(NS_STEPS):
        x_wide = ortho_bf.astype(jnp.float32)
        square = jnp.einsum('bij,bkj->bik', x_wide, x_wide).astype(jnp.bfloat16)
        square_wide = square.astype(jnp.float32)
        quartic = jnp.einsum('bij,bjk->bik', square_wide, square_wide)
        mixer_bf = (ns_cubic * square_wide + ns_quintic * quartic).astype(jnp.bfloat16)
        ortho_bf = (ns_linear * x_wide + jnp.einsum('bij,bjk->bik', mixer_bf.astype(jnp.float32), x_wide)).astype(jnp.bfloat16)
    return ortho_bf

def reference(attn_q, attn_k, attn_v, step_size, fast_init, boundary, window_len):
    attended = window_attention(attn_q, attn_k, attn_v, window_len)
    in_first = jnp.arange(TOKENS, dtype=jnp.int32) < boundary[0]
    outputs = []
    for head_id in range(FH):
        col_lo = head_id * FW
        fast_q = rms_norm(attn_q[:, col_lo:col_lo + FW]).astype(jnp.bfloat16)
        fast_k = rms_norm(attn_k[:, col_lo:col_lo + FW]).astype(jnp.bfloat16)
        fast_v = attn_v[:, col_lo:col_lo + FW]
        weights = fast_init[head_id]
        result = jnp.zeros((TOKENS, FW), jnp.float32)
        for section_id in range(2):
            inside = in_first if section_id == 0 else jnp.logical_not(in_first)
            token_scale = step_size[head_id] * inside.astype(jnp.float32)
            grad_sum = swiglu_grads(fast_k, fast_v, token_scale, weights)
            weights = weights + newton_schulz(grad_sum).astype(jnp.float32)
            result = jnp.where(inside[:, None], swiglu_apply(fast_q, weights), result)
        combined = attended[:, col_lo:col_lo + FW].astype(jnp.float32) + rms_norm(result)
        outputs.append(combined.astype(jnp.bfloat16))
    return jnp.concatenate(outputs, axis=1)
```

```python
import math

import jax
import jax.numpy as jnp
from jax import lax
from jax.sharding import Mesh
from jax.sharding import PartitionSpec as P

AH = 128
NS_STEPS = 2
CTX_AXES = ("y", "zl", "x", "c")
CHIP_AXES = ("y", "zl", "x")
SPLIT = (4, 2, 4, 2)

ns_linear = 3.4445
ns_cubic = -4.775
ns_quintic = 2.0315


def rms_norm(values):
    x_wide = values.astype(jnp.float32)
    return x_wide / jnp.sqrt(jnp.mean(x_wide * x_wide, axis=-1, keepdims=True) + 1e-06)


def attend_local(queries, key_rows, value_rows, window_len, first_pos, block):
    tokens = queries.shape[0]
    n_heads = queries.shape[1] // AH
    outs = []
    for b in range(tokens // block):
        q_split = queries[b * block : (b + 1) * block].reshape(block, n_heads, AH)
        k_split = key_rows[b * block : (b + 2) * block].reshape(2 * block, n_heads, AH)
        v_split = value_rows[b * block : (b + 2) * block].reshape(2 * block, n_heads, AH)
        scores = jnp.einsum(
            "qhd,khd->hqk", q_split, k_split, preferred_element_type=jnp.float32
        ) / math.sqrt(AH)
        q_pos = first_pos + b * block + jnp.arange(block, dtype=jnp.int32)
        k_pos = first_pos + (b - 1) * block + jnp.arange(2 * block, dtype=jnp.int32)
        pos_gap = q_pos[:, None] - k_pos[None, :]
        allowed = (
            (pos_gap[None] >= 0)
            & (pos_gap[None] < window_len[:, None, None])
            & (k_pos[None, None, :] >= 0)
        )
        masked = jnp.where(allowed, scores, -jnp.inf)
        row_peak = jnp.max(masked, axis=-1, keepdims=True)
        expo_val = jnp.exp(masked - row_peak)
        weights_bf = (expo_val / jnp.sum(expo_val, axis=-1, keepdims=True)).astype(jnp.bfloat16)
        mixed = jnp.einsum("hqk,khd->qhd", weights_bf, v_split, preferred_element_type=jnp.float32)
        outs.append(mixed.reshape(block, n_heads * AH).astype(jnp.bfloat16))
    return jnp.concatenate(outs, axis=0)


def swiglu_grads(fast_k, fast_v, token_scale, w_bf):
    pre_gate = jnp.dot(fast_k, w_bf[0], preferred_element_type=jnp.float32)
    pre_up = jnp.dot(fast_k, w_bf[1], preferred_element_type=jnp.float32)
    gate_sig = jax.nn.sigmoid(pre_gate)
    gate_act = pre_gate * gate_sig
    hidden = (gate_act * pre_up).astype(jnp.bfloat16)
    target = (fast_v.astype(jnp.float32) * token_scale[:, None]).astype(jnp.bfloat16)
    over_rows = (((0,), (0,)), ((), ()))
    grad_down = lax.dot_general(hidden, target, over_rows, preferred_element_type=jnp.float32)
    back_out = lax.dot_general(
        target, w_bf[2], (((1,), (1,)), ((), ())), preferred_element_type=jnp.float32
    )
    back_gate = (back_out * pre_up * gate_sig * (1.0 + pre_gate * (1.0 - gate_sig))).astype(
        jnp.bfloat16
    )
    back_up = (back_out * gate_act).astype(jnp.bfloat16)
    grad_gate = lax.dot_general(fast_k, back_gate, over_rows, preferred_element_type=jnp.float32)
    grad_up = lax.dot_general(fast_k, back_up, over_rows, preferred_element_type=jnp.float32)
    return jnp.concatenate([grad_gate, grad_up, grad_down], axis=0)


def swiglu_apply(fast_q, w_bf):
    pre_gate = jnp.dot(fast_q, w_bf[0], preferred_element_type=jnp.float32)
    pre_up = jnp.dot(fast_q, w_bf[1], preferred_element_type=jnp.float32)
    hidden = (pre_gate * jax.nn.sigmoid(pre_gate) * pre_up).astype(jnp.bfloat16)
    return jnp.dot(hidden, w_bf[2], preferred_element_type=jnp.float32)


def newton_schulz(grad_sum):
    norm_sq = jnp.sum(grad_sum * grad_sum, axis=(1, 2))
    ortho_bf = (grad_sum / (jnp.sqrt(norm_sq) + 1e-07)[:, None, None]).astype(jnp.bfloat16)
    for ns_step in range(NS_STEPS):
        square = jnp.einsum(
            "bij,bkj->bik", ortho_bf, ortho_bf, preferred_element_type=jnp.float32
        ).astype(jnp.bfloat16)
        quartic = jnp.einsum("bij,bjk->bik", square, square, preferred_element_type=jnp.float32)
        mixer_bf = (ns_cubic * square.astype(jnp.float32) + ns_quintic * quartic).astype(
            jnp.bfloat16
        )
        applied = jnp.einsum("bij,bjk->bik", mixer_bf, ortho_bf, preferred_element_type=jnp.float32)
        ortho_bf = (ns_linear * ortho_bf.astype(jnp.float32) + applied).astype(jnp.bfloat16)
    return ortho_bf


def swap_cores(x):
    return lax.ppermute(x, "c", [(0, 1), (1, 0)])


def sum_over_ctx(partial):
    rows, cols = partial.shape
    half = cols // 2
    core = lax.axis_index("c")
    mine = lax.dynamic_slice_in_dim(partial, core * half, half, 1)
    theirs = lax.dynamic_slice_in_dim(partial, (1 - core) * half, half, 1)
    got = swap_cores(theirs.astype(jnp.bfloat16))
    pair_sum = (mine + got.astype(jnp.float32)).astype(jnp.bfloat16)
    chips = SPLIT[0] * SPLIT[1] * SPLIT[2]
    pieces = lax.all_to_all(
        pair_sum.reshape(chips, rows // chips, half), CHIP_AXES, 0, 0, tiled=True
    )
    total = jnp.sum(pieces.astype(jnp.float32), axis=0).astype(jnp.bfloat16)
    spread = jnp.broadcast_to(total[None], (chips, rows // chips, half))
    whole = lax.all_to_all(spread, CHIP_AXES, 0, 0, tiled=True).reshape(rows, half)
    other = swap_cores(whole)
    first = jnp.where(core == 0, whole, other)
    second = jnp.where(core == 0, other, whole)
    return jnp.concatenate([first, second], axis=1)


def local(attn_q, attn_k, attn_v, step_size, fast_init, boundary, window_len):
    heads = lax.axis_size("zh")
    head = lax.axis_index("zh")
    ctx = lax.axis_index(CTX_AXES)
    block, width = attn_q.shape
    fw = width // heads

    def by_head(x):
        return jnp.swapaxes(x.reshape(block, heads, fw), 0, 1)

    kv = jnp.stack([by_head(attn_k), by_head(attn_v)], axis=1)
    kv = lax.all_to_all(kv, "zh", 0, 0, tiled=True)
    fast_kin = kv[:, 0].reshape(heads * block, fw)
    fast_v = kv[:, 1].reshape(heads * block, fw)
    fast_qin = lax.all_to_all(by_head(attn_q), "zh", 0, 0, tiled=True).reshape(heads * block, fw)
    tok_count = heads * block
    n_ctx = lax.axis_size(CTX_AXES)
    halo = lax.ppermute(kv[heads - 1], CTX_AXES, [(i, i + 1) for i in range(n_ctx - 1)])
    att_heads = fw // AH
    my_windows = lax.dynamic_slice_in_dim(window_len, head * att_heads, att_heads)
    attended = attend_local(
        fast_qin,
        jnp.concatenate([halo[0], fast_kin], axis=0),
        jnp.concatenate([halo[1], fast_v], axis=0),
        my_windows,
        ctx * tok_count,
        block,
    )
    query_bf = rms_norm(fast_qin).astype(jnp.bfloat16)
    key_bf = rms_norm(fast_kin).astype(jnp.bfloat16)
    positions = ctx * tok_count + jnp.arange(tok_count, dtype=jnp.int32)
    in_first = positions < boundary[0]
    weights = fast_init[0]
    result = jnp.zeros((tok_count, fw), jnp.float32)
    for section_id in range(2):
        inside = in_first if section_id == 0 else jnp.logical_not(in_first)
        token_scale = step_size[0] * inside.astype(jnp.float32)
        partial_value = swiglu_grads(key_bf, fast_v, token_scale, weights.astype(jnp.bfloat16))
        grad_sum = sum_over_ctx(partial_value).reshape(3, fw, fw).astype(jnp.float32)
        weights = weights + newton_schulz(grad_sum).astype(jnp.float32)
        applied = swiglu_apply(query_bf, weights.astype(jnp.bfloat16))
        result = jnp.where(inside[:, None], applied, result)
    return (attended.astype(jnp.float32) + rms_norm(result)).astype(jnp.bfloat16)


def solution(mesh):
    heads = mesh.devices.shape[1]
    fine = Mesh(mesh.devices.reshape(SPLIT + (heads,)), CTX_AXES + ("zh",))
    tokens = CTX_AXES + ("zh",)
    return jax.shard_map(
        local,
        mesh=fine,
        in_specs=(
            P(tokens, None),
            P(tokens, None),
            P(tokens, None),
            P("zh", CTX_AXES),
            P("zh", None, None, None),
            P(),
            P(),
        ),
        out_specs=P(CTX_AXES, "zh"),
        check_vma=False,
    )
```

```python
import math

import jax
import jax.numpy as jnp
from jax import lax
from jax.experimental import pallas as pl
from jax.experimental.pallas import tpu as pltpu
from jax.sharding import Mesh
from jax.sharding import PartitionSpec as P

AH = 128
NS_STEPS = 2
FW = 512
HALF = FW // 2
HEADS = 4
BLK = 128
TOK = HEADS * BLK
CTX_AXES = ("y", "zl", "x", "c")
CHIP_AXES = ("y", "zl", "x")
SPLIT = (4, 2, 4, 2)
CHIPS = 32
ROWS = 3 * FW
PIECE = ROWS // CHIPS

ns_linear = 3.4445
ns_cubic = -4.775
ns_quintic = 2.0315

F32 = jnp.float32
BF = jnp.bfloat16
NN = (((1,), (0,)), ((), ()))
NT = (((1,), (1,)), ((), ()))
TN = (((0,), (0,)), ((), ()))


def dot(a, b, dims=NN):
    return lax.dot_general(a, b, dims, preferred_element_type=F32)


def vmem():
    return pl.BlockSpec(memory_space=pltpu.VMEM)


def smem():
    return pl.BlockSpec(memory_space=pltpu.SMEM)


def call(body, ins, outs, scratch=(), name=None, flops=0, limit=24, trans=0):
    size = sum(math.prod(s) * jnp.dtype(d).itemsize for s, d in outs)
    specs = [smem() if x.dtype == jnp.int32 else vmem() for x in ins]
    return pl.pallas_call(
        body,
        out_shape=[jax.ShapeDtypeStruct(s, d) for s, d in outs],
        in_specs=specs,
        out_specs=[vmem() for _ in outs],
        scratch_shapes=[pltpu.VMEM(s, d) for s, d in scratch],
        compiler_params=pltpu.CompilerParams(vmem_limit_bytes=limit << 20),
        cost_estimate=pl.CostEstimate(
            flops=flops, bytes_accessed=2 * size, transcendentals=trans
        ),
        name=name,
    )(*ins)


def half_at(core):
    return pl.ds(pl.multiple_of(core * HALF, HALF), HALF)


def rms(x):
    return x / jnp.sqrt(jnp.mean(x * x, axis=-1, keepdims=True) + 1e-06)


def pack_kv(k_ref, v_ref, *outs):
    head = lax.axis_index("zh")
    for s in range(HEADS):
        cols = pl.ds(pl.multiple_of(lax.rem(head + s, HEADS) * FW, FW), FW)
        outs[s][0:BLK, :] = k_ref[:, cols]
        outs[s][BLK : 2 * BLK, :] = v_ref[:, cols]


def pack_q(q_ref, out):
    for s in range(HEADS):
        out[s] = q_ref[:, s * FW : (s + 1) * FW]


def grads(kbf, kt, v, scale, w, hid, bg, bu, tg, mine, theirs):
    core = lax.axis_index("c")
    step = 256
    for b in range(TOK // step):
        rows = pl.ds(b * step, step)
        kb = kbf[rows, :]
        sc = scale[rows, :]
        target = (v[rows, :].astype(F32) * jnp.concatenate([sc] * (FW // 128), axis=1)).astype(BF)
        tg[rows, :] = target
        back_out = dot(target, w[2], NT)
        gate = dot(kb, w[0])
        up = dot(kb, w[1])
        sig = jax.nn.sigmoid(gate)
        act = gate * sig
        hid[rows, :] = (act * up).astype(BF)
        bg[rows, :] = (back_out * up * sig * (1.0 + gate * (1.0 - sig))).astype(BF)
        bu[rows, :] = (back_out * act).astype(BF)
    for out, which in ((theirs, 1 - core), (mine, core)):
        cols = half_at(which)
        out[0:FW, :] = dot(kt[...], bg[:, cols]).astype(out.dtype)
        out[FW : 2 * FW, :] = dot(kt[...], bu[:, cols]).astype(out.dtype)
        out[2 * FW : 3 * FW, :] = dot(hid[...], tg[:, cols], TN).astype(out.dtype)


def first_grads(
    p0, p1, p2, p3, scale, w0, mine, theirs, kraw, vout, kbf, kt, halo, wb, hid, bg, bu, tg
):
    head = lax.axis_index("zh")
    for s, piece in enumerate((p0, p1, p2, p3)):
        rows = pl.ds(pl.multiple_of(lax.rem(head - s + HEADS, HEADS) * BLK, BLK), BLK)
        kraw[rows, :] = piece[0:BLK, :]
        vout[rows, :] = piece[BLK : 2 * BLK, :]
        kbf[rows, :] = rms(piece[0:BLK, :].astype(F32)).astype(BF)
    halo[0:BLK, :] = kraw[TOK - BLK : TOK, :]
    halo[BLK : 2 * BLK, :] = vout[TOK - BLK : TOK, :]
    kt[...] = kbf[...].T
    for i in range(3):
        wb[i] = w0[i].astype(BF)
    grads(kbf, kt, vout, scale, wb, hid, bg, bu, tg, mine, theirs)


def add_pair(mine, got, out):
    out[...] = (mine[...] + got[...].astype(F32)).astype(BF)


def sum_chips(pieces, out):
    total = pieces[0:PIECE, :].astype(F32)
    for j in range(1, CHIPS):
        total = total + pieces[j * PIECE : (j + 1) * PIECE, :].astype(F32)
    total = total.astype(BF)
    for j in range(CHIPS):
        out[j * PIECE : (j + 1) * PIECE, :] = total


def newton_schulz(whole, other, x_ref, a_ref, finish):
    core = lax.axis_index("c")

    def one(i, carry):
        rows = pl.ds(pl.multiple_of(i * FW, FW), FW)
        g0 = whole[rows, :].astype(F32)
        g1 = other[rows, :].astype(F32)
        norm_sq = jnp.sum(g0 * g0 + g1 * g1, keepdims=True)
        inv = 1.0 / (jnp.sqrt(norm_sq) + 1e-07)
        x_ref[:, half_at(core)] = (g0 * inv).astype(BF)
        x_ref[:, half_at(1 - core)] = (g1 * inv).astype(BF)
        for _ in range(NS_STEPS):
            x = x_ref[...]
            a_ref[...] = dot(x, x, NT).astype(BF)
            a = a_ref[...]
            mixer = (ns_cubic * a.astype(F32) + ns_quintic * dot(a, a)).astype(BF)
            x_ref[...] = (ns_linear * x.astype(F32) + dot(mixer, x)).astype(BF)
        finish(i, x_ref[...])
        return carry

    lax.fori_loop(0, 3, one, 0)


def second_grads(
    whole, other, w0, kbf, kt, v, scale, mine, theirs, wb, x1, x_ref, a_ref, hid, bg, bu, tg
):
    def finish(i, x):
        x1[i] = x
        wb[i] = (w0[i] + x.astype(F32)).astype(BF)

    newton_schulz(whole, other, x_ref, a_ref, finish)
    grads(kbf, kt, v, scale, wb, hid, bg, bu, tg, mine, theirs)


def apply_rows(qbf, w):
    gate = dot(qbf, w[0])
    up = dot(qbf, w[1])
    hidden = (gate * jax.nn.sigmoid(gate) * up).astype(BF)
    return rms(dot(hidden, w[2]))


def attend(q_ref, kraw, v, halo, window_len, att, qbf, kx, vx):
    head = lax.axis_index("zh")
    ctx = lax.axis_index(CTX_AXES)
    kx[0:BLK, :] = halo[0:BLK, :]
    vx[0:BLK, :] = halo[BLK : 2 * BLK, :]
    kx[BLK:, :] = kraw[...]
    vx[BLK:, :] = v[...]
    qbf[...] = rms(q_ref[...].astype(F32)).astype(BF)
    row = lax.broadcasted_iota(jnp.int32, (BLK, 2 * BLK), 0)
    col = lax.broadcasted_iota(jnp.int32, (BLK, 2 * BLK), 1)
    gap = row - col + BLK
    scale = 1.0 / math.sqrt(AH)
    per = FW // AH
    for a in range(per):
        cols = slice(a * AH, (a + 1) * AH)
        near = (gap >= 0) & (gap < window_len[head * per + a])

        def one(b, carry):
            rows = pl.ds(pl.multiple_of(b * BLK, BLK), BLK)
            keys = pl.ds(pl.multiple_of(b * BLK, BLK), 2 * BLK)
            allowed = near & (col >= BLK - (ctx * TOK + b * BLK))
            score = dot(q_ref[rows, cols], kx[keys, cols], NT) * scale
            score = jnp.where(allowed, score, -1e30)
            e = jnp.exp(score - jnp.max(score, axis=-1, keepdims=True))
            weight = (e / jnp.sum(e, axis=-1, keepdims=True)).astype(BF)
            att[rows, cols] = dot(weight, vx[keys, cols]).astype(BF)
            return carry

        lax.fori_loop(0, TOK // BLK, one, 0)


def first_apply(qbf, wb, att, out):
    step = 256
    for b in range(TOK // step):
        rows = pl.ds(b * step, step)
        out[rows, :] = (att[rows, :].astype(F32) + apply_rows(qbf[rows, :], wb)).astype(BF)


def last_apply(whole, other, w0, x1, qbf, att, out1, boundary, out, x_ref, a_ref, wb):
    def finish(i, x):
        wb[i] = (w0[i] + x1[i].astype(F32) + x.astype(F32)).astype(BF)

    newton_schulz(whole, other, x_ref, a_ref, finish)
    base = lax.axis_index(CTX_AXES) * TOK
    step = 256
    for b in range(TOK // step):
        rows = pl.ds(b * step, step)
        mixed = (att[rows, :].astype(F32) + apply_rows(qbf[rows, :], wb)).astype(F32)
        pos = base + b * step + lax.broadcasted_iota(jnp.int32, (step, FW), 0)
        kept = out1[rows, :].astype(F32)
        out[rows, :] = jnp.where(pos < boundary[0], kept, mixed).astype(BF)


def swap_cores(x):
    return lax.ppermute(x, "c", [(0, 1), (1, 0)])


MM = 2 * FW * FW * FW
SQ = (FW, FW)
TOKS = (TOK, FW)
HALVES = (ROWS, HALF)
KINDS = (3, FW, FW)


def sum_over_ctx(mine, theirs):
    got = swap_cores(theirs)
    (pair,) = call(add_pair, [mine, got], [(HALVES, BF)], name="add_pair")
    pieces = lax.all_to_all(pair.reshape(CHIPS, PIECE, HALF), CHIP_AXES, 0, 0, tiled=True)
    (spread,) = call(sum_chips, [pieces.reshape(HALVES)], [(HALVES, BF)], name="sum_chips")
    whole = lax.all_to_all(spread.reshape(CHIPS, PIECE, HALF), CHIP_AXES, 0, 0, tiled=True)
    whole = whole.reshape(HALVES)
    return whole, swap_cores(whole)


def local(attn_q, attn_k, attn_v, step_size, fast_init, boundary, window_len):
    ctx = lax.axis_index(CTX_AXES)
    w0 = fast_init[0]
    packed = call(pack_kv, [attn_k, attn_v], [((2 * BLK, FW), BF)] * HEADS, name="pack_kv")
    pieces = [packed[0]]
    got = {}
    for s in (2, 1, 3):
        got[s] = lax.ppermute(packed[s], "zh", [(i, (i + s) % HEADS) for i in range(HEADS)])
    pieces += [got[1], got[2], got[3]]
    positions = ctx * TOK + jnp.arange(TOK, dtype=jnp.int32)
    in_first = (positions < boundary[0]).astype(F32)
    scale1 = jnp.broadcast_to((step_size[0] * in_first)[:, None], (TOK, 128))
    scale2 = jnp.broadcast_to((step_size[0] * (1.0 - in_first))[:, None], (TOK, 128))
    (q_send,) = call(pack_q, [attn_q], [((HEADS, BLK, FW), BF)], name="pack_q")

    four = [(TOKS, BF)] * 4
    mine, theirs, kraw, v, kbf, kt, halo_out = call(
        first_grads,
        pieces + [scale1, w0],
        [(HALVES, F32), (HALVES, BF), (TOKS, BF), (TOKS, BF), (TOKS, BF), (SQ, BF)]
        + [((2 * BLK, FW), BF)],
        [(KINDS, BF)] + four,
        name="first_grads",
        flops=6 * MM,
    )
    q = lax.all_to_all(q_send, "zh", 0, 0, tiled=True).reshape(TOKS)
    n_ctx = lax.axis_size(CTX_AXES)
    halo = lax.ppermute(halo_out, CTX_AXES, [(i, i + 1) for i in range(n_ctx - 1)])
    att, qbf = call(
        attend,
        [q, kraw, v, halo, window_len],
        [(TOKS, BF), (TOKS, BF)],
        [((TOK + BLK, FW), BF)] * 2,
        name="attend",
        flops=2 * MM,
        trans=TOK * FW * 2,
    )
    whole, other = sum_over_ctx(mine, theirs)
    mine, theirs, wb1, x1 = call(
        second_grads,
        [whole, other, w0, kbf, kt, v, scale2],
        [(HALVES, F32), (HALVES, BF), (KINDS, BF), (KINDS, BF)],
        [(SQ, BF), (SQ, BF)] + four,
        name="second_grads",
        flops=24 * MM,
    )
    (out1,) = call(first_apply, [qbf, wb1, att], [(TOKS, BF)], name="first_apply", flops=3 * MM)
    whole, other = sum_over_ctx(mine, theirs)
    (out,) = call(
        last_apply,
        [whole, other, w0, x1, qbf, att, out1, boundary],
        [(TOKS, BF)],
        [(SQ, BF), (SQ, BF), (KINDS, BF)],
        name="last_apply",
        flops=21 * MM,
    )
    return out


def solution(mesh):
    heads = mesh.devices.shape[1]
    fine = Mesh(mesh.devices.reshape(SPLIT + (heads,)), CTX_AXES + ("zh",))
    tokens = CTX_AXES + ("zh",)
    return jax.shard_map(
        local,
        mesh=fine,
        in_specs=(
            P(tokens, None),
            P(tokens, None),
            P(tokens, None),
            P("zh", CTX_AXES),
            P("zh", None, None, None),
            P(),
            P(),
        ),
        out_specs=P(CTX_AXES, "zh"),
        check_vma=False,
    )
```
